32 devices in a mesh: dp: 16 (over z, y, x), section: 2 (over core).
Axes of the slice: x: 2, y: 2, z: 4, core: 2. Of those that a mesh axis runs over, the one named last changes fastest.
Arguments:
- path_table: bfloat16 [512, 2048], replicated, may hold values from -6 to 6
- tokens: int32 [16, 8, 48], P('dp'), may hold values from 0 to 511
- assign: int32 [16, 8], P('dp'), may hold values from 0 to 7, each once within a row
- out_grad: bfloat16 [16, 2, 4, 48, 2048], P('dp'), may hold values from -6 to 6
- query_weights: bfloat16 [2, 2048, 128], P('section', 'dp'), may hold values from -1 to 24
- gain: bfloat16 [2, 2048], P('section', 'dp'), may hold values from 0.5 to 1.5
- scale: bfloat16 [2, 2048], P('section', 'dp'), may hold values from 0.14 to 1.82
Outputs:
- query_grad: float32 [2, 2048, 128], P('section', 'dp')
- gain_grad: float32 [2, 2048], P('section', 'dp')
- scale_grad: float32 [2, 2048], P('section', 'dp')
The draws below stay inside these ranges and needn't reach their ends.
All inputs are finite; a program needn't handle non-finite values.
Results may differ from the reference program's by a relative error of at most 0.0031.
Values may be sent and summed in bfloat16 or wider, within the bound.
A program may use at most 64 MiB of HBM per device.

```python
import math
import jax
import jax.numpy as jnp
import numpy as np
from jax import lax

D = 2048
HD = 128
VOCAB = 512
SEQ = 48
MICRO = 4
BLOCKS = 2
N_DP = 16


def shared_offset(key):
    offset_key = jax.random.fold_in(key, 7001)
    magnitude = jax.random.uniform(jax.random.fold_in(offset_key, 1), (D,), jnp.float32, 0.3, 0.6)
    flipped = jax.random.bernoulli(jax.random.fold_in(offset_key, 2), 0.5, (D,))
    return magnitude * jnp.where(flipped, 1.0, -1.0)


def draw_path_table(key, part):
    own_key = jax.random.fold_in(key, 11)
    values = jax.random.truncated_normal(own_key, -5.0, 5.0, (VOCAB, D), jnp.float32)
    return (values + shared_offset(key)[None, :]).astype(jnp.bfloat16)


def draw_out_grad(key, part):
    own_key = jax.random.fold_in(key, 13)
    shape_full = (N_DP, 2, MICRO, SEQ, D)
    values = jax.random.truncated_normal(own_key, -5.0, 5.0, shape_full, jnp.float32)
    return (values + shared_offset(key)[None, None, None, None, :]).astype(jnp.bfloat16)


def draw_query_weights(key, part):
    base = jax.random.truncated_normal(key, -3.0, 3.0, (BLOCKS, D, HD), jnp.float32) * HD ** (-0.5)
    return base.astype(jnp.bfloat16)


def draw_scale(key, part):
    level = jnp.arange(BLOCKS, dtype=jnp.float32) / (BLOCKS - 1)
    rising = 0.3 * jnp.power(3.0, level)
    jitter = jnp.exp(jax.random.uniform(key, (BLOCKS, D), jnp.float32, -0.69, 0.69))
    return (rising[:, None] * jitter).astype(jnp.bfloat16)


def plant(array, rng, least, high):
    dims = array.shape
    index_at = [jax.random.randint(jax.random.fold_in(rng, axis), (), 0, dims[axis]) for axis in range(len(dims))]
    array = array.at[tuple(index_at)].set(least)
    longest = dims.index(max(dims))
    index_at[longest] = (index_at[longest] + 1) % dims[longest]
    return array.at[tuple(index_at)].set(high)


def rank_table(amount, lean):
    portions = [(1 << 20) // math.isqrt(grade ** lean) + 1 for grade in range(1, amount + 1)]
    spread = 1 + sum(portions) // (1 << 30)
    return np.cumsum(np.array([max(1, weight // spread) for weight in portions]))


def ranked_ids(key, shape, number_of, slope):
    table = rank_table(number_of, slope)
    lot = jax.random.randint(jax.random.fold_in(key, 1), shape, 0, int(table[number_of - 1]))
    grade = jnp.searchsorted(jnp.asarray(table, jnp.int32), lot, side="right")
    return jax.random.permutation(jax.random.fold_in(key, 2), number_of)[grade].astype(jnp.int32)


def setup_inputs(seed: int = 0) -> dict:
    arg_keys = jax.random.split(jax.random.key(seed), 8)
    return {
        "path_table": draw_path_table(jax.random.fold_in(arg_keys[7], 71), 0),
        "tokens": plant(ranked_ids(arg_keys[1], (N_DP, 2 * MICRO, SEQ), VOCAB, 2), jax.random.fold_in(arg_keys[1], 3), 0, VOCAB - 1).astype(jnp.int32),
        "assign": jax.vmap(lambda own: jax.random.permutation(own, 2 * MICRO))(jax.random.split(arg_keys[2], N_DP)).reshape((N_DP, 2 * MICRO)).astype(jnp.int32),
        "out_grad": draw_out_grad(jax.random.fold_in(arg_keys[7], 71), 0),
        "query_weights": draw_query_weights(jax.random.fold_in(arg_keys[7], 71), 0),
        "gain": jnp.clip(1.0 + 0.1 * jax.random.normal(arg_keys[5], (BLOCKS, D), jnp.float32), 0.5, 1.5).astype(jnp.bfloat16),
        "scale": draw_scale(jax.random.fold_in(arg_keys[7], 71), 0),
    }


HIGH = lax.Precision.HIGHEST

def block_apply(stream_in, query_map, gain_vec, scale_vec):
    batch_count, seq_len, model_width = stream_in.shape
    head_size = query_map.shape[1]
    head_count = model_width // head_size
    stream = stream_in.astype(jnp.float32)
    mean_square = lax.optimization_barrier(jnp.mean(stream * stream, axis=-1, keepdims=True))
    normed = stream * lax.rsqrt(mean_square + 1e-05) * gain_vec
    normed = lax.optimization_barrier(normed.astype(jnp.bfloat16)).astype(jnp.float32)
    heads_in = normed.reshape(batch_count, seq_len, head_count, head_size)
    query_heads = query_map.reshape(head_count, head_size, head_size)
    queries = jnp.einsum('nshi,hij->nshj', heads_in, query_heads, precision=HIGH) * (1.0 / math.sqrt(head_size))
    queries = lax.optimization_barrier(queries.astype(jnp.bfloat16)).astype(jnp.float32)
    scores = jnp.einsum('nshj,nthj->nhst', queries, heads_in, precision=HIGH)
    causal = lax.broadcasted_iota(jnp.int32, (seq_len, seq_len), 0) >= lax.broadcasted_iota(jnp.int32, (seq_len, seq_len), 1)
    scores = jnp.where(causal, scores, -1e+30)
    row_max = lax.optimization_barrier(jnp.max(scores, axis=-1, keepdims=True))
    raised = jnp.exp(scores - row_max)
    attend = raised / lax.optimization_barrier(jnp.sum(raised, axis=-1, keepdims=True))
    attend = lax.optimization_barrier(attend.astype(jnp.bfloat16)).astype(jnp.float32)
    mixed = jnp.einsum('nhst,nthj->nshj', attend, heads_in, precision=HIGH).reshape(batch_count, seq_len, model_width)
    return (stream + scale_vec * mixed).astype(jnp.bfloat16)

def reference(path_table, tokens, assign, out_grad, query_weights, gain, scale):
    slot_tokens = jnp.take_along_axis(tokens, assign[:, :, None].astype(jnp.int32), axis=1)
    start_stream = jnp.take(path_table, slot_tokens.reshape(-1, SEQ), axis=0)
    params = (query_weights.astype(jnp.float32), gain.astype(jnp.float32), scale.astype(jnp.float32))

    def model(layer_params):
        stream = start_stream
        for block_index in range(BLOCKS):
            stream = block_apply(stream, layer_params[0][block_index], layer_params[1][block_index], layer_params[2][block_index])
        return stream
    final_stream, pullback = jax.vjp(model, params)
    (query_raw, gain_raw, scale_raw), = pullback(out_grad.reshape(final_stream.shape))
    total = jnp.sum(query_raw * query_raw) + jnp.sum(gain_raw * gain_raw) + jnp.sum(scale_raw * scale_raw)
    factor = jnp.minimum(1.0, math.sqrt(float(BLOCKS * D * (HD + 2))) / jnp.sqrt(total))
    return (query_raw * factor, gain_raw * factor, scale_raw * factor)
```

```python
import functools
import math

import jax
import jax.numpy as jnp
from jax import lax
from jax.experimental import pallas as pl
from jax.experimental.pallas import tpu as pltpu
from jax.sharding import PartitionSpec as P

MESH = pl.DeviceIdType.MESH
F32 = jnp.float32
BF16 = jnp.bfloat16
TAIL = 16
GROUP = 2


def matmul(lhs, rhs, lhs_dim, rhs_dim):
    return lax.dot_general(
        lhs, rhs, (((lhs_dim,), (rhs_dim,)), ((), ())), preferred_element_type=F32
    )


def step_kernel(
    n_dp,
    n_sec,
    table,
    tokens,
    assign,
    out_grad,
    weights,
    gain,
    scale,
    query_out,
    gain_out,
    scale_out,
    packed,
    params,
    picked,
    tbl,
    cot,
    xs,
    normed,
    queries,
    mixed,
    probs,
    dnormed,
    acc,
    rstd,
    parts,
    tx,
    rx,
    norms,
    load_sem,
    w_send,
    w_recv,
    x_send,
    x_recv,
    g_send,
    g_recv,
    n_send,
    n_recv,
):
    slots, seq = tokens.shape
    heads, count, hd = cot.shape
    vocab, width = table.shape
    rows = weights.shape[0]
    layers = n_sec
    pieces = n_dp // n_sec
    per_head = hd // rows
    n_dev = n_dp * n_sec
    group_rows = GROUP * seq
    groups = slots // GROUP
    inv = 1.0 / math.sqrt(hd)
    me_d = lax.axis_index("dp")
    me_s = lax.axis_index("section")
    me = me_d * n_sec + me_s

    def columns(h):
        return pl.ds(pl.multiple_of((me_s * heads + h) * hd, hd), hd)

    def remote(src, dst, ssem, rsem, d, s):
        return pltpu.make_async_remote_copy(
            src_ref=src,
            dst_ref=dst,
            send_sem=ssem,
            recv_sem=rsem,
            device_id=(d, s),
            device_id_type=MESH,
        )

    for h in range(heads):
        pltpu.make_async_copy(table.at[:, columns(h)], tbl.at[h], load_sem.at[0]).start()
    for h in range(heads):
        pltpu.make_async_copy(out_grad.at[:, columns(h)], cot.at[h], load_sem.at[1]).start()

    barrier = pltpu.get_barrier_semaphore()

    def greet(k, carry):
        t = lax.rem(me + k, n_dev)
        pl.semaphore_signal(
            barrier,
            inc=1,
            device_id=(lax.div(t, n_sec), lax.rem(t, n_sec)),
            device_id_type=MESH,
        )
        return carry

    lax.fori_loop(1, n_dev, greet, 0)

    packed[0:rows, :] = weights[...]
    tail_row = lax.broadcasted_iota(jnp.int32, (TAIL, hd), 0)
    packed[rows : rows + TAIL, :] = jnp.where(
        tail_row == 0,
        gain[...].astype(F32),
        jnp.where(tail_row == 1, scale[...].astype(F32), 0.0),
    ).astype(BF16)

    eye = lax.broadcasted_iota(jnp.int32, (seq, seq), 0) == lax.broadcasted_iota(
        jnp.int32, (seq, seq), 1
    )
    vocab_lane = lax.broadcasted_iota(jnp.int32, (seq, vocab), 1).astype(F32)
    for j in range(slots):
        row = tokens[pl.ds(assign[j], 1), :].astype(F32)
        col = jnp.sum(jnp.where(eye, row, 0.0), axis=1, keepdims=True)
        picked[j * seq : (j + 1) * seq, :] = jnp.where(vocab_lane == col, 1.0, 0.0).astype(BF16)

    pl.semaphore_wait(barrier, n_dev - 1)

    owner = lax.div(me_d, pieces)
    place = lax.rem(me_d, pieces)
    keep = owner == me_s

    @pl.when(keep)
    def _():
        pltpu.make_async_copy(packed, params.at[me_s, place], w_recv.at[me_s]).start()

    @pl.when(jnp.logical_not(keep))
    def _():
        remote(packed, params.at[me_s, place], w_send, w_recv.at[me_s], me_d, owner).start()

    def give(k, carry):
        r = lax.rem(me_d + k, n_dp)
        remote(packed, params.at[me_s, place], w_send, w_recv.at[me_s], r, owner).start()
        return carry

    lax.fori_loop(1, n_dp, give, 0)

    lane = lax.broadcasted_iota(jnp.int32, (seq, hd), 1)

    def exchange(phase):
        sums = jnp.sum(acc[...], axis=1, keepdims=True)
        compact = jnp.zeros((seq, hd), F32)
        for j in range(slots):
            compact = jnp.where(lane == j, sums[j * seq : (j + 1) * seq], compact)
        parts[phase, pl.ds(me_s, 1)] = compact[None]
        for k in range(1, n_sec):
            s = lax.rem(me_s + k, n_sec)
            remote(
                parts.at[phase, me_s], parts.at[phase, me_s], x_send, x_recv.at[phase], me_d, s
            ).start()

    def exchanged(phase):
        if n_sec > 1:
            whole = parts.at[phase, pl.ds(0, n_sec - 1)]
            pltpu.make_async_copy(whole, whole, x_recv.at[phase]).wait()
        return jnp.sum(parts[phase], axis=0)

    def spread(compact, j):
        return jnp.broadcast_to(compact[:, j : j + 1], (seq, hd))

    def layer_param(b, h):
        block = params[b, pl.ds(h * per_head, per_head)]
        if per_head == 1:
            tail = block[0, rows:, :].astype(F32)
            weight = block[0, :rows, :]
        else:
            tail = block[0, rows:, :].astype(F32)
            for i in range(1, per_head):
                tail = tail + block[i, rows:, :].astype(F32)
            weight = jnp.concatenate([block[i, :rows, :] for i in range(per_head)], axis=0)
        return weight, tail[0:1], tail[1:2]

    pltpu.make_async_copy(tbl, tbl, load_sem.at[0]).wait()
    acc[...] = jnp.zeros_like(acc)

    def embed(h, carry):
        rows_in = matmul(picked[...], tbl[h], 1, 0)
        xs[0, h] = rows_in.astype(BF16)
        acc[...] += rows_in * rows_in
        return carry

    lax.fori_loop(0, heads, embed, 0)

    at_row = lax.broadcasted_iota(jnp.int32, (group_rows, group_rows), 0)
    at_col = lax.broadcasted_iota(jnp.int32, (group_rows, group_rows), 1)
    allowed = at_row >= at_col
    for i in range(1, GROUP):
        allowed = allowed & ((at_row >= i * seq) == (at_col >= i * seq))

    for b in range(layers):
        exchange(b)
        if b == 0:
            for i in range(layers):
                pltpu.make_async_copy(params.at[i], params.at[i], w_recv.at[i]).wait()
        root = lax.rsqrt(exchanged(b) * (1.0 / width) + 1e-05)
        for j in range(slots):
            rstd[b, j * seq : (j + 1) * seq, :] = spread(root, j)
        acc[...] = jnp.zeros_like(acc)

        def forward(h, carry):
            weight, gain_row, scale_row = layer_param(b, h)
            x_in = xs[b, h].astype(F32)
            norm = (x_in * rstd[b] * gain_row).astype(BF16)
            normed[b, h] = norm
            query = (matmul(norm, weight, 1, 0) * inv).astype(BF16)
            queries[b, h] = query
            for i in range(groups):
                lo, hi = i * group_rows, (i + 1) * group_rows
                scores = matmul(query[lo:hi], norm[lo:hi], 1, 1)
                scores = jnp.where(allowed, scores, -1e30)
                raised = jnp.exp(scores - jnp.max(scores, axis=1, keepdims=True))
                attend = raised * (1.0 / jnp.sum(raised, axis=1, keepdims=True))
                probs[b, h, i] = attend
                mix = matmul(attend.astype(BF16), norm[lo:hi], 1, 0)
                mixed[b, h, lo:hi] = mix
                if b + 1 < layers:
                    out = (x_in[lo:hi] + scale_row * mix).astype(BF16)
                    xs[b + 1, h, lo:hi] = out
                    out = out.astype(F32)
                    acc[lo:hi] += out * out
            return carry

        lax.fori_loop(0, heads, forward, 0)

    pltpu.make_async_copy(cot, cot, load_sem.at[1]).wait()

    for b in reversed(range(layers)):
        if b > 0:
            acc[...] = jnp.zeros_like(acc)

        def backward(h, carry):
            weight, gain_row, scale_row = layer_param(b, h)
            given = cot[h].astype(F32)
            scale_part = jnp.sum(given * mixed[b, h], axis=0, keepdims=True)
            norm = normed[b, h]
            query = queries[b, h]
            dmix = (given * scale_row).astype(BF16)
            dquery_parts, dnorm_parts = [], []
            for i in range(groups):
                lo, hi = i * group_rows, (i + 1) * group_rows
                attend = probs[b, h, i]
                dattend = matmul(dmix[lo:hi], norm[lo:hi], 1, 1).astype(BF16).astype(F32)
                inner = jnp.sum(dattend * attend, axis=1, keepdims=True)
                dscore = (attend * (dattend - inner)).astype(BF16)
                dquery_parts.append(matmul(dscore, norm[lo:hi], 1, 0).astype(BF16))
                left = jnp.concatenate([dscore, attend.astype(BF16)], axis=0)
                right = jnp.concatenate([query[lo:hi], dmix[lo:hi]], axis=0)
                dnorm_parts.append(matmul(left, right, 0, 0))
            dquery = jnp.concatenate(dquery_parts, axis=0)
            dnorm = jnp.concatenate(dnorm_parts, axis=0) + matmul(dquery, weight, 1, 1) * inv
            dweight = matmul(norm, dquery, 0, 0) * inv
            dnorm = dnorm.astype(BF16)
            if b > 0:
                dnormed[h] = dnorm
            dnorm = dnorm.astype(F32)
            x_in = xs[b, h].astype(F32)
            gain_part = jnp.sum(dnorm * (x_in * rstd[b]), axis=0, keepdims=True)
            if b > 0:
                acc[...] += dnorm * gain_row * x_in
            gain_hi = gain_part.astype(BF16).astype(F32)
            scale_hi = scale_part.astype(BF16).astype(F32)
            tail = jnp.where(
                tail_row == 0,
                gain_hi,
                jnp.where(
                    tail_row == 1,
                    gain_part - gain_hi,
                    jnp.where(
                        tail_row == 2,
                        scale_hi,
                        jnp.where(tail_row == 3, scale_part - scale_hi, 0.0),
                    ),
                ),
            ).astype(BF16)
            dweight = dweight.astype(BF16)
            for i in range(per_head):
                p = h * per_head + i
                tx[b, p, 0:rows] = dweight[i * rows : (i + 1) * rows]
                tx[b, p, rows : rows + TAIL] = tail
                r = me_s * pieces + p
                mine = (r == me_d) & (me_s == b)

                @pl.when(mine)
                def _():
                    pltpu.make_async_copy(tx.at[b, p], rx.at[me_d], g_recv).start()

                @pl.when(jnp.logical_not(mine))
                def _():
                    remote(tx.at[b, p], rx.at[me_d], g_send, g_recv, r, b).start()

            return carry

        lax.fori_loop(0, heads, backward, 0)
        if b > 0:
            phase = layers + b - 1
            exchange(phase)
            inner = exchanged(phase) * (1.0 / width)
            acc_rows = [spread(inner, j) for j in range(slots)]
            root = rstd[b]
            acc[...] = jnp.concatenate(acc_rows, axis=0) * root * root * root

            def stream_back(h, carry):
                _, gain_row, _ = layer_param(b, h)
                dy = dnormed[h].astype(F32) * gain_row
                back = rstd[b] * dy - xs[b, h].astype(F32) * acc[...]
                cot[h] = (cot[h].astype(F32) + back).astype(BF16)
                return carry

            lax.fori_loop(0, heads, stream_back, 0)

    pltpu.make_async_copy(rx, rx, g_recv).wait()
    total = jnp.sum(rx[...].astype(F32), axis=0)
    total_query = total[0:rows]
    total_gain = total[rows : rows + 1] + total[rows + 1 : rows + 2]
    total_scale = total[rows + 2 : rows + 3] + total[rows + 3 : rows + 4]
    if per_head > 1:
        at = lax.broadcasted_iota(jnp.int32, (1, hd), 1)
        first = lax.rem(me_d, per_head) * rows
        inside = (at >= first) & (at < first + rows)
        total_gain = jnp.where(inside, total_gain, 0.0)
        total_scale = jnp.where(inside, total_scale, 0.0)
    squares = (
        jnp.sum(total_query * total_query, axis=0, keepdims=True)
        + total_gain * total_gain
        + total_scale * total_scale
    )
    norms[pl.ds(me, 1)] = squares[None]

    def tell(k, carry):
        t = lax.rem(me + k, n_dev)
        remote(
            norms.at[me], norms.at[me], n_send, n_recv, lax.div(t, n_sec), lax.rem(t, n_sec)
        ).start()
        return carry

    lax.fori_loop(1, n_dev, tell, 0)
    others = norms.at[pl.ds(0, n_dev - 1)]
    pltpu.make_async_copy(others, others, n_recv).wait()
    overall = jnp.sum(jnp.sum(norms[...], axis=0), axis=1, keepdims=True)
    limit = float(layers * width * (hd + 2))
    factor = jnp.minimum(1.0, math.sqrt(limit) / jnp.sqrt(overall))
    query_out[...] = total_query * factor
    gain_out[...] = total_gain * factor
    scale_out[...] = total_scale * factor

    pltpu.make_async_copy(others, others, n_send).wait()
    if n_sec > 1:
        for phase in range(2 * layers - 1):
            whole = parts.at[phase, pl.ds(0, n_sec - 1)]
            pltpu.make_async_copy(whole, whole, x_send).wait()

    def sent_weight(k, carry):
        pltpu.make_async_copy(packed, packed, w_send).wait()
        return carry

    lax.fori_loop(0, jnp.where(keep, n_dp - 1, n_dp), sent_weight, 0)

    def sent_grad(k, carry):
        pltpu.make_async_copy(packed, packed, g_send).wait()
        return carry

    lax.fori_loop(0, jnp.where(keep, layers * pieces - 1, layers * pieces), sent_grad, 0)


def on_device(path_table, tokens, assign, out_grad, query_weights, gain, scale):
    n_dp = lax.axis_size("dp")
    n_sec = lax.axis_size("section")
    vocab, width = path_table.shape
    slots, seq = tokens.shape[1:]
    rows, hd = query_weights.shape[1:]
    count = slots * seq
    layers = n_sec
    heads = width // n_sec // hd
    pieces = n_dp // n_sec
    n_dev = n_dp * n_sec
    groups = slots // GROUP
    first = lax.rem(lax.axis_index("dp") * rows, hd)
    if rows < hd:
        gain = lax.dynamic_update_slice(jnp.zeros((1, hd), BF16), gain, (0, first))
        scale = lax.dynamic_update_slice(jnp.zeros((1, hd), BF16), scale, (0, first))
    vmem = pl.BlockSpec(memory_space=pltpu.VMEM)
    hbm = pl.BlockSpec(memory_space=pl.ANY)
    smem = pl.BlockSpec(memory_space=pltpu.SMEM)
    query_grad, gain_grad, scale_grad = pl.pallas_call(
        functools.partial(step_kernel, n_dp, n_sec),
        out_shape=(
            jax.ShapeDtypeStruct((rows, hd), F32),
            jax.ShapeDtypeStruct((1, hd), F32),
            jax.ShapeDtypeStruct((1, hd), F32),
        ),
        in_specs=[hbm, vmem, smem, hbm, vmem, vmem, vmem],
        out_specs=(vmem, vmem, vmem),
        scratch_shapes=[
            pltpu.VMEM((rows + TAIL, hd), BF16),
            pltpu.VMEM((layers, pieces, rows + TAIL, hd), BF16),
            pltpu.VMEM((count, vocab), BF16),
            pltpu.VMEM((heads, vocab, hd), BF16),
            pltpu.VMEM((heads, count, hd), BF16),
            pltpu.VMEM((layers, heads, count, hd), BF16),
            pltpu.VMEM((layers, heads, count, hd), BF16),
            pltpu.VMEM((layers, heads, count, hd), BF16),
            pltpu.VMEM((layers, heads, count, hd), F32),
            pltpu.VMEM((layers, heads, groups, GROUP * seq, GROUP * seq), F32),
            pltpu.VMEM((heads, count, hd), BF16),
            pltpu.VMEM((count, hd), F32),
            pltpu.VMEM((layers, count, hd), F32),
            pltpu.VMEM((2 * layers - 1, n_sec, seq, hd), F32),
            pltpu.VMEM((layers, pieces, rows + TAIL, hd), BF16),
            pltpu.VMEM((n_dp, rows + TAIL, hd), BF16),
            pltpu.VMEM((n_dev, 1, hd), F32),
            pltpu.SemaphoreType.DMA((2,)),
            pltpu.SemaphoreType.DMA,
            pltpu.SemaphoreType.DMA((layers,)),
            pltpu.SemaphoreType.DMA,
            pltpu.SemaphoreType.DMA((2 * layers - 1,)),
            pltpu.SemaphoreType.DMA,
            pltpu.SemaphoreType.DMA,
            pltpu.SemaphoreType.DMA,
            pltpu.SemaphoreType.DMA,
        ],
        compiler_params=pltpu.CompilerParams(
            collective_id=0, has_side_effects=True, vmem_limit_bytes=56 * 1024 * 1024
        ),
    )(
        path_table,
        tokens[0],
        assign[0],
        out_grad.reshape(count, width),
        query_weights[0],
        gain,
        scale,
    )
    if rows < hd:
        gain_grad = lax.dynamic_slice(gain_grad, (0, first), (1, rows))
        scale_grad = lax.dynamic_slice(scale_grad, (0, first), (1, rows))
    return query_grad[None], gain_grad, scale_grad


def solution(mesh):
    in_specs = (
        P(),
        P("dp", None, None),
        P("dp", None),
        P("dp", None, None, None, None),
        P("section", "dp", None),
        P("section", "dp"),
        P("section", "dp"),
    )
    out_specs = (P("section", "dp", None), P("section", "dp"), P("section", "dp"))
    return jax.shard_map(
        on_device, mesh=mesh, in_specs=in_specs, out_specs=out_specs, check_vma=False
    )
```

```python
import functools
import math

import jax
import jax.numpy as jnp
from jax import lax
from jax.experimental import pallas as pl
from jax.experimental.pallas import tpu as pltpu
from jax.sharding import PartitionSpec as P

MESH = pl.DeviceIdType.MESH
F32 = jnp.float32
BF16 = jnp.bfloat16
TAIL = 16
GROUP = 2
PLANE = 4


def matmul(lhs, rhs, lhs_dim, rhs_dim):
    return lax.dot_general(
        lhs, rhs, (((lhs_dim,), (rhs_dim,)), ((), ())), preferred_element_type=F32
    )


def layout(n_dp, n_sec, width, hd):
    plane = math.gcd(n_dp, min(PLANE, width // hd // n_sec))
    return plane, n_dp // plane, width // hd // n_sec // plane


def step_kernel(
    n_dp,
    n_sec,
    table,
    tokens,
    assign,
    out_grad,
    weights,
    gain,
    scale,
    query_out,
    gain_out,
    scale_out,
    packed,
    params,
    toks,
    picked,
    tbl,
    emb,
    cot,
    xs,
    normed,
    queries,
    mixed,
    probs,
    dnormed,
    acc,
    rstd,
    parts,
    grads,
    tails,
    tx,
    rx,
    norms,
    load_sem,
    t_send,
    t_recv,
    w_send,
    w_recv,
    c_send,
    c_recv,
    x_send,
    x_recv,
    g_send,
    g_recv,
    n_send,
    n_recv,
):
    slots, seq = tokens.shape
    vocab, width = table.shape
    rows, hd = weights.shape
    plane, planes, heads = layout(n_dp, n_sec, width, hd)
    layers = n_sec
    per_head = hd // rows
    n_dev = n_dp * n_sec
    members = plane * n_sec
    group_rows = GROUP * seq
    groups = slots // GROUP
    inv = 1.0 / math.sqrt(hd)
    me_d = lax.axis_index("dp")
    me_s = lax.axis_index("section")
    me = me_d * n_sec + me_s
    me_z = lax.div(me_d, plane)
    me_p = lax.rem(me_d, plane)
    member = me_p * n_sec + me_s

    def head_of(p, c, hh):
        return (c * heads + hh) * plane + p

    def columns(h):
        return pl.ds(pl.multiple_of(h * hd, hd), hd)

    def remote(src, dst, ssem, rsem, d, s):
        return pltpu.make_async_remote_copy(
            src_ref=src,
            dst_ref=dst,
            send_sem=ssem,
            recv_sem=rsem,
            device_id=(d, s),
            device_id_type=MESH,
        )

    pltpu.make_async_copy(table, tbl, load_sem).start()
    for hh in range(heads):
        pltpu.make_async_copy(
            out_grad.at[:, columns(head_of(me_p, me_s, hh))], cot.at[me_p, hh], c_recv.at[me_p]
        ).start()

    barrier = pltpu.get_barrier_semaphore()

    def greet(k, carry):
        t = lax.rem(me + k, n_dev)
        pl.semaphore_signal(
            barrier,
            inc=1,
            device_id=(lax.div(t, n_sec), lax.rem(t, n_sec)),
            device_id_type=MESH,
        )
        return carry

    lax.fori_loop(1, n_dev, greet, 0)

    packed[0:rows, :] = weights[...]
    tail_row = lax.broadcasted_iota(jnp.int32, (TAIL, hd), 0)
    packed[rows : rows + TAIL, :] = jnp.where(
        tail_row == 0,
        gain[...].astype(F32),
        jnp.where(tail_row == 1, scale[...].astype(F32), 0.0),
    ).astype(BF16)
    for j in range(slots):
        toks[me_p, j : j + 1, 0:seq] = tokens[pl.ds(assign[j], 1), :].astype(F32)

    pltpu.make_async_copy(tbl, tbl, load_sem).wait()
    chunk = math.gcd(vocab, 64)
    lane_chunk = lax.broadcasted_iota(jnp.int32, (chunk, hd), 1)

    def table_norm(i, carry):
        at = pl.ds(pl.multiple_of(i * chunk, chunk), chunk)
        squares = jnp.zeros((chunk, hd), F32)
        for h in range(width // hd):
            block = tbl[at, h * hd : (h + 1) * hd].astype(F32)
            squares = squares + block * block
        root = lax.rsqrt(jnp.sum(squares, axis=1, keepdims=True) * (1.0 / width) + 1e-05)
        high = root.astype(BF16).astype(F32)
        mid = (root - high).astype(BF16).astype(F32)
        low = root - high - mid
        emb[at, heads * hd : (heads + 1) * hd] = jnp.where(
            lane_chunk == 0,
            high,
            jnp.where(lane_chunk == 1, mid, jnp.where(lane_chunk == 2, low, 0.0)),
        ).astype(BF16)
        return carry

    lax.fori_loop(0, vocab // chunk, table_norm, 0)
    for hh in range(heads):
        emb[:, hh * hd : (hh + 1) * hd] = tbl[:, columns(head_of(me_p, me_s, hh))]

    pl.semaphore_wait(barrier, n_dev - 1)

    for k in range(1, plane):
        p = lax.rem(me_p + k, plane)
        remote(toks.at[me_p], toks.at[me_p], t_send, t_recv, me_z * plane + p, me_s).start()

    my_head = lax.div(me_d * rows, hd)
    to_p = lax.rem(my_head, plane)
    to_i = lax.div(my_head, plane)
    to_s = lax.div(to_i, heads)
    place = lax.rem(to_i, heads) * per_head + lax.rem(me_d, per_head)
    keep = (to_p == me_p) & (to_s == me_s)

    @pl.when(keep)
    def _():
        pltpu.make_async_copy(packed, params.at[me_s, place], w_recv.at[me_s]).start()

    @pl.when(jnp.logical_not(keep))
    def _():
        remote(
            packed,
            params.at[me_s, place],
            w_send,
            w_recv.at[me_s],
            me_z * plane + to_p,
            to_s,
        ).start()

    def give(k, carry):
        z = lax.rem(me_z + k, planes)
        remote(
            packed, params.at[me_s, place], w_send, w_recv.at[me_s], z * plane + to_p, to_s
        ).start()
        return carry

    lax.fori_loop(1, planes, give, 0)

    for k in range(1, plane):
        p = lax.rem(me_p + k, plane)
        for hh in range(heads):
            remote(
                out_grad.at[:, columns(head_of(p, me_s, hh))],
                cot.at[me_p, hh],
                c_send,
                c_recv.at[me_p],
                me_z * plane + p,
                me_s,
            ).start()

    eye = lax.broadcasted_iota(jnp.int32, (seq, seq), 0) == lax.broadcasted_iota(
        jnp.int32, (seq, seq), 1
    )

    def as_column(row):
        return jnp.sum(jnp.where(eye, row, 0.0), axis=1, keepdims=True)

    def exchange(phase, q):
        sums = jnp.sum(acc[...], axis=1, keepdims=True)
        for j in range(slots):
            own = jnp.where(eye, sums[j * seq : (j + 1) * seq], 0.0)
            parts[phase, q, member, j : j + 1, 0:seq] = jnp.sum(own, axis=0, keepdims=True)

        def share(k, carry):
            t = lax.rem(member + k, members)
            remote(
                parts.at[phase, q, member],
                parts.at[phase, q, member],
                x_send,
                x_recv.at[phase, q],
                me_z * plane + lax.div(t, n_sec),
                lax.rem(t, n_sec),
            ).start()
            return carry

        lax.fori_loop(1, members, share, 0)

    def exchanged(phase, q):
        if members > 1:
            whole = parts.at[phase, q, pl.ds(0, members - 1)]
            pltpu.make_async_copy(whole, whole, x_recv.at[phase, q]).wait()
        return jnp.sum(parts[phase, q, :, :, 0:seq], axis=0)

    def layer_param(b, hh):
        at = hh * per_head
        tail = params[b, at, rows:, :].astype(F32)
        weight = params[b, at, :rows, :]
        if per_head > 1:
            for i in range(1, per_head):
                tail = tail + params[b, at + i, rows:, :].astype(F32)
            weight = jnp.concatenate(
                [params[b, at + i, :rows, :] for i in range(per_head)], axis=0
            )
        return weight, tail[0:1], tail[1:2]

    at_row = lax.broadcasted_iota(jnp.int32, (group_rows, group_rows), 0)
    at_col = lax.broadcasted_iota(jnp.int32, (group_rows, group_rows), 1)
    allowed = at_row <= at_col
    for i in range(1, GROUP):
        allowed = allowed & ((at_row >= i * seq) == (at_col >= i * seq))
    vocab_lane = lax.broadcasted_iota(jnp.int32, (seq, vocab), 1).astype(F32)

    if plane > 1:
        pltpu.make_async_copy(
            toks.at[pl.ds(0, plane - 1)], toks.at[pl.ds(0, plane - 1)], t_recv
        ).wait()

    def embed(q, carry):
        for j in range(slots):
            col = as_column(toks[q, j : j + 1, 0:seq])
            picked[j * seq : (j + 1) * seq, :] = jnp.where(vocab_lane == col, 1.0, 0.0).astype(
                BF16
            )
        found = matmul(picked[...], emb[...], 1, 0)
        for hh in range(heads):
            xs[0, q, hh] = found[:, hh * hd : (hh + 1) * hd].astype(BF16)
        root = jnp.sum(found[:, heads * hd :], axis=1, keepdims=True)
        rstd[0, q] = jnp.broadcast_to(root, (slots * seq, hd))
        return carry

    lax.fori_loop(0, plane, embed, 0)
    for i in range(layers):
        pltpu.make_async_copy(params.at[i], params.at[i], w_recv.at[i]).wait()

    for b in range(layers):

        def forward(q, carry):
            if b > 0:
                root = lax.rsqrt(exchanged(b - 1, q) * (1.0 / width) + 1e-05)
                for j in range(slots):
                    rstd[b, q, j * seq : (j + 1) * seq, :] = jnp.broadcast_to(
                        as_column(root[j : j + 1]), (seq, hd)
                    )
            for hh in range(heads):
                weight, gain_row, scale_row = layer_param(b, hh)
                x_in = xs[b, q, hh].astype(F32)
                norm = (x_in * rstd[b, q] * gain_row).astype(BF16)
                normed[b, q, hh] = norm
                query = (matmul(norm, weight, 1, 0) * inv).astype(BF16)
                queries[b, q, hh] = query
                for i in range(groups):
                    lo, hi = i * group_rows, (i + 1) * group_rows
                    scores = matmul(norm[lo:hi], query[lo:hi], 1, 1)
                    scores = jnp.where(allowed, scores, -1e30)
                    raised = jnp.exp(scores - jnp.max(scores, axis=0, keepdims=True))
                    attend = raised * (1.0 / jnp.sum(raised, axis=0, keepdims=True))
                    probs[b, q, hh, i] = attend
                    mix = matmul(attend.astype(BF16), norm[lo:hi], 0, 0)
                    mixed[b, q, hh, lo:hi] = mix
                    if b + 1 < layers:
                        out = (x_in[lo:hi] + scale_row * mix).astype(BF16)
                        xs[b + 1, q, hh, lo:hi] = out
                        out = out.astype(F32)
                        if hh == 0:
                            acc[lo:hi] = out * out
                        else:
                            acc[lo:hi] += out * out
            if b + 1 < layers:
                exchange(b, q)
            return carry

        lax.fori_loop(0, plane, forward, 0)

    for b in reversed(range(layers)):
        for hh in range(heads):
            grads[hh] = jnp.zeros((hd, hd), F32)
            tails[hh] = jnp.zeros((8, hd), F32)

        def backward(q, carry):
            if b + 1 == layers:
                pltpu.make_async_copy(cot.at[q], cot.at[q], c_recv.at[q]).wait()
            else:
                phase = layers - 1 + b
                inner = exchanged(phase, q) * (1.0 / width)
                for j in range(slots):
                    at = slice(j * seq, (j + 1) * seq)
                    root = rstd[b + 1, q, at]
                    acc[at] = as_column(inner[j : j + 1]) * root * root * root
                for hh in range(heads):
                    _, gain_row, _ = layer_param(b + 1, hh)
                    dy = dnormed[q, hh].astype(F32) * gain_row
                    back = rstd[b + 1, q] * dy - xs[b + 1, q, hh].astype(F32) * acc[...]
                    cot[q, hh] = (cot[q, hh].astype(F32) + back).astype(BF16)
            for hh in range(heads):
                weight, gain_row, scale_row = layer_param(b, hh)
                given = cot[q, hh].astype(F32)
                scale_part = jnp.sum(given * mixed[b, q, hh], axis=0, keepdims=True)
                norm = normed[b, q, hh]
                query = queries[b, q, hh]
                dmix = (given * scale_row).astype(BF16)
                dquery_parts, dnorm_parts = [], []
                for i in range(groups):
                    lo, hi = i * group_rows, (i + 1) * group_rows
                    attend = probs[b, q, hh, i]
                    dattend = matmul(norm[lo:hi], dmix[lo:hi], 1, 1).astype(BF16).astype(F32)
                    inner = jnp.sum(dattend * attend, axis=0, keepdims=True)
                    dscore = (attend * (dattend - inner)).astype(BF16)
                    dquery_parts.append(matmul(dscore, norm[lo:hi], 0, 0).astype(BF16))
                    dnorm_parts.append(
                        matmul(dscore, query[lo:hi], 1, 0)
                        + matmul(attend.astype(BF16), dmix[lo:hi], 1, 0)
                    )
                dquery = jnp.concatenate(dquery_parts, axis=0)
                dnorm = jnp.concatenate(dnorm_parts, axis=0) + matmul(dquery, weight, 1, 1) * inv
                grads[hh] += matmul(norm, dquery, 0, 0)
                dnorm = dnorm.astype(BF16)
                if b > 0:
                    dnormed[q, hh] = dnorm
                dnorm = dnorm.astype(F32)
                x_in = xs[b, q, hh].astype(F32)
                tails[hh, 0:1] += jnp.sum(dnorm * (x_in * rstd[b, q]), axis=0, keepdims=True)
                tails[hh, 1:2] += scale_part
                if b > 0:
                    inside = dnorm * gain_row * x_in
                    if hh == 0:
                        acc[...] = inside
                    else:
                        acc[...] += inside
            if b > 0:
                exchange(layers - 2 + b, q)
            return carry

        lax.fori_loop(0, plane, backward, 0)
        for hh in range(heads):
            gain_part, scale_part = tails[hh, 0:1], tails[hh, 1:2]
            gain_hi = gain_part.astype(BF16).astype(F32)
            scale_hi = scale_part.astype(BF16).astype(F32)
            tail = jnp.where(
                tail_row == 0,
                gain_hi,
                jnp.where(
                    tail_row == 1,
                    gain_part - gain_hi,
                    jnp.where(
                        tail_row == 2,
                        scale_hi,
                        jnp.where(tail_row == 3, scale_part - scale_hi, 0.0),
                    ),
                ),
            ).astype(BF16)
            dweight = (grads[hh] * inv).astype(BF16)
            for i in range(per_head):
                at = hh * per_head + i
                tx[b, at, 0:rows] = dweight[i * rows : (i + 1) * rows]
                tx[b, at, rows : rows + TAIL] = tail
        for hh in range(heads):
            for i in range(per_head):
                at = hh * per_head + i
                r = head_of(me_p, me_s, hh) * per_head + i
                mine = (r == me_d) & (me_s == b)

                @pl.when(mine)
                def _():
                    pltpu.make_async_copy(tx.at[b, at], rx.at[me_z], g_recv).start()

                @pl.when(jnp.logical_not(mine))
                def _():
                    remote(tx.at[b, at], rx.at[me_z], g_send, g_recv, r, b).start()

    pltpu.make_async_copy(rx, rx, g_recv).wait()
    total = jnp.sum(rx[...].astype(F32), axis=0)
    total_query = total[0:rows]
    total_gain = total[rows : rows + 1] + total[rows + 1 : rows + 2]
    total_scale = total[rows + 2 : rows + 3] + total[rows + 3 : rows + 4]
    if per_head > 1:
        at = lax.broadcasted_iota(jnp.int32, (1, hd), 1)
        first = lax.rem(me_d, per_head) * rows
        inside = (at >= first) & (at < first + rows)
        total_gain = jnp.where(inside, total_gain, 0.0)
        total_scale = jnp.where(inside, total_scale, 0.0)
    squares = (
        jnp.sum(total_query * total_query, axis=0, keepdims=True)
        + total_gain * total_gain
        + total_scale * total_scale
    )
    norms[pl.ds(me, 1)] = squares[None]

    def tell(k, carry):
        t = lax.rem(me + k, n_dev)
        remote(
            norms.at[me], norms.at[me], n_send, n_recv, lax.div(t, n_sec), lax.rem(t, n_sec)
        ).start()
        return carry

    lax.fori_loop(1, n_dev, tell, 0)
    others = norms.at[pl.ds(0, n_dev - 1)]
    pltpu.make_async_copy(others, others, n_recv).wait()
    overall = jnp.sum(jnp.sum(norms[...], axis=0), axis=1, keepdims=True)
    limit = float(layers * width * (hd + 2))
    factor = jnp.minimum(1.0, math.sqrt(limit) / jnp.sqrt(overall))
    query_out[...] = total_query * factor
    gain_out[...] = total_gain * factor
    scale_out[...] = total_scale * factor

    pltpu.make_async_copy(others, others, n_send).wait()
    if members > 1:
        for phase in range(2 * layers - 2):
            whole = parts.at[phase, :, pl.ds(0, members - 1)]
            pltpu.make_async_copy(whole, whole, x_send).wait()
    if plane > 1:
        sent = toks.at[pl.ds(0, plane - 1)]
        pltpu.make_async_copy(sent, sent, t_send).wait()
        sent = cot.at[pl.ds(0, plane - 1)]
        pltpu.make_async_copy(sent, sent, c_send).wait()

    def sent_weight(k, carry):
        pltpu.make_async_copy(packed, packed, w_send).wait()
        return carry

    lax.fori_loop(0, jnp.where(keep, planes - 1, planes), sent_weight, 0)

    def sent_grad(k, carry):
        pltpu.make_async_copy(packed, packed, g_send).wait()
        return carry

    pieces = layers * heads * per_head
    lax.fori_loop(0, jnp.where(keep, pieces - 1, pieces), sent_grad, 0)


def on_device(path_table, tokens, assign, out_grad, query_weights, gain, scale):
    n_dp = lax.axis_size("dp")
    n_sec = lax.axis_size("section")
    vocab, width = path_table.shape
    slots, seq = tokens.shape[1:]
    rows, hd = query_weights.shape[1:]
    count = slots * seq
    layers = n_sec
    plane, planes, heads = layout(n_dp, n_sec, width, hd)
    per_head = hd // rows
    pieces = heads * per_head
    n_dev = n_dp * n_sec
    groups = slots // GROUP
    first = lax.rem(lax.axis_index("dp") * rows, hd)
    if rows < hd:
        gain = lax.dynamic_update_slice(jnp.zeros((1, hd), BF16), gain, (0, first))
        scale = lax.dynamic_update_slice(jnp.zeros((1, hd), BF16), scale, (0, first))
    vmem = pl.BlockSpec(memory_space=pltpu.VMEM)
    hbm = pl.BlockSpec(memory_space=pl.ANY)
    smem = pl.BlockSpec(memory_space=pltpu.SMEM)
    query_grad, gain_grad, scale_grad = pl.pallas_call(
        functools.partial(step_kernel, n_dp, n_sec),
        out_shape=(
            jax.ShapeDtypeStruct((rows, hd), F32),
            jax.ShapeDtypeStruct((1, hd), F32),
            jax.ShapeDtypeStruct((1, hd), F32),
        ),
        in_specs=[hbm, vmem, smem, hbm, vmem, vmem, vmem],
        out_specs=(vmem, vmem, vmem),
        scratch_shapes=[
            pltpu.VMEM((rows + TAIL, hd), BF16),
            pltpu.VMEM((layers, pieces, rows + TAIL, hd), BF16),
            pltpu.VMEM((plane, slots, hd), F32),
            pltpu.VMEM((count, vocab), BF16),
            pltpu.VMEM((vocab, width), BF16),
            pltpu.VMEM((vocab, (heads + 1) * hd), BF16),
            pltpu.VMEM((plane, heads, count, hd), BF16),
            pltpu.VMEM((layers, plane, heads, count, hd), BF16),
            pltpu.VMEM((layers, plane, heads, count, hd), BF16),
            pltpu.VMEM((layers, plane, heads, count, hd), BF16),
            pltpu.VMEM((layers, plane, heads, count, hd), F32),
            pltpu.VMEM((layers, plane, heads, groups, GROUP * seq, GROUP * seq), F32),
            pltpu.VMEM((plane, heads, count, hd), BF16),
            pltpu.VMEM((count, hd), F32),
            pltpu.VMEM((layers, plane, count, hd), F32),
            pltpu.VMEM((max(1, 2 * layers - 2), plane, plane * n_sec, slots, hd), F32),
            pltpu.VMEM((heads, hd, hd), F32),
            pltpu.VMEM((heads, 8, hd), F32),
            pltpu.VMEM((layers, pieces, rows + TAIL, hd), BF16),
            pltpu.VMEM((planes, rows + TAIL, hd), BF16),
            pltpu.VMEM((n_dev, 1, hd), F32),
            pltpu.SemaphoreType.DMA,
            pltpu.SemaphoreType.DMA,
            pltpu.SemaphoreType.DMA,
            pltpu.SemaphoreType.DMA,
            pltpu.SemaphoreType.DMA((layers,)),
            pltpu.SemaphoreType.DMA,
            pltpu.SemaphoreType.DMA((plane,)),
            pltpu.SemaphoreType.DMA,
            pltpu.SemaphoreType.DMA((max(1, 2 * layers - 2), plane)),
            pltpu.SemaphoreType.DMA,
            pltpu.SemaphoreType.DMA,
            pltpu.SemaphoreType.DMA,
            pltpu.SemaphoreType.DMA,
        ],
        compiler_params=pltpu.CompilerParams(
            collective_id=0, has_side_effects=True, vmem_limit_bytes=56 * 1024 * 1024
        ),
    )(
        path_table,
        tokens[0],
        assign[0],
        out_grad.reshape(count, width),
        query_weights[0],
        gain,
        scale,
    )
    if rows < hd:
        gain_grad = lax.dynamic_slice(gain_grad, (0, first), (1, rows))
        scale_grad = lax.dynamic_slice(scale_grad, (0, first), (1, rows))
    return query_grad[None], gain_grad, scale_grad


def solution(mesh):
    in_specs = (
        P(),
        P("dp", None, None),
        P("dp", None),
        P("dp", None, None, None, None),
        P("section", "dp", None),
        P("section", "dp"),
        P("section", "dp"),
    )
    out_specs = (P("section", "dp", None), P("section", "dp"), P("section", "dp"))
    return jax.shard_map(
        on_device, mesh=mesh, in_specs=in_specs, out_specs=out_specs, check_vma=False
    )
```

```python
import functools
import math

import jax
import jax.numpy as jnp
from jax import lax
from jax.experimental import pallas as pl
from jax.experimental.pallas import tpu as pltpu
from jax.sharding import PartitionSpec as P

MESH = pl.DeviceIdType.MESH
F32 = jnp.float32
BF16 = jnp.bfloat16
TAIL = 16
GROUP = 2
PLANE = 4
AHEAD = 4


def matmul(lhs, rhs, lhs_dim, rhs_dim):
    return lax.dot_general(
        lhs, rhs, (((lhs_dim,), (rhs_dim,)), ((), ())), preferred_element_type=F32
    )


def layout(n_dp, n_sec, width, hd):
    plane = math.gcd(n_dp, min(PLANE, width // hd // n_sec))
    return plane, n_dp // plane, width // hd // n_sec // plane


def step_kernel(
    n_dp,
    n_sec,
    table,
    tokens,
    assign,
    out_grad,
    weights,
    gain,
    scale,
    out,
    packed,
    params,
    toks,
    picked,
    tbl,
    emb,
    cot,
    xs,
    normed,
    queries,
    mixed,
    probs,
    dnormed,
    acc,
    rstd,
    parts,
    grads,
    tails,
    tx,
    rx,
    norms,
    load_sem,
    t_send,
    t_recv,
    w_send,
    w_recv,
    c_send,
    c_recv,
    x_send,
    x_recv,
    g_send,
    g_recv,
    n_send,
    n_recv,
):
    slots, seq = tokens.shape
    vocab, width = table.shape
    rows, hd = weights.shape
    plane, planes, heads = layout(n_dp, n_sec, width, hd)
    layers = n_sec
    per_head = hd // rows
    n_dev = n_dp * n_sec
    members = plane * n_sec
    group_rows = GROUP * seq
    groups = slots // GROUP
    inv = 1.0 / math.sqrt(hd)
    me_d = lax.axis_index("dp")
    me_s = lax.axis_index("section")
    me = me_d * n_sec + me_s
    me_z = lax.div(me_d, plane)
    me_p = lax.rem(me_d, plane)
    member = me_p * n_sec + me_s

    def head_of(p, c, hh):
        return (c * heads + hh) * plane + p

    def columns(h):
        return pl.ds(pl.multiple_of(h * hd, hd), hd)

    def remote(src, dst, ssem, rsem, d, s):
        return pltpu.make_async_remote_copy(
            src_ref=src,
            dst_ref=dst,
            send_sem=ssem,
            recv_sem=rsem,
            device_id=(d, s),
            device_id_type=MESH,
        )

    pltpu.make_async_copy(table, tbl, load_sem).start()
    for hh in range(heads):
        pltpu.make_async_copy(
            out_grad.at[:, columns(head_of(me_p, me_s, hh))], cot.at[me_p, hh], c_recv.at[me_p]
        ).start()

    barrier = pltpu.get_barrier_semaphore()

    def greet(k, carry):
        t = lax.rem(me + k, n_dev)
        pl.semaphore_signal(
            barrier,
            inc=1,
            device_id=(lax.div(t, n_sec), lax.rem(t, n_sec)),
            device_id_type=MESH,
        )
        return carry

    lax.fori_loop(1, n_dev, greet, 0)

    packed[0:rows, :] = weights[...]
    tail_row = lax.broadcasted_iota(jnp.int32, (TAIL, hd), 0)
    packed[rows : rows + TAIL, :] = jnp.where(
        tail_row == 0,
        gain[...].astype(F32),
        jnp.where(tail_row == 1, scale[...].astype(F32), 0.0),
    ).astype(BF16)
    for j in range(slots):
        toks[me_p, j : j + 1, 0:seq] = tokens[pl.ds(assign[j], 1), :].astype(F32)

    pltpu.make_async_copy(tbl, tbl, load_sem).wait()
    chunk = math.gcd(vocab, 64)
    lane_chunk = lax.broadcasted_iota(jnp.int32, (chunk, hd), 1)

    def table_norm(i, carry):
        at = pl.ds(pl.multiple_of(i * chunk, chunk), chunk)
        squares = jnp.zeros((chunk, hd), F32)
        for h in range(width // hd):
            block = tbl[at, h * hd : (h + 1) * hd].astype(F32)
            squares = squares + block * block
        root = lax.rsqrt(jnp.sum(squares, axis=1, keepdims=True) * (1.0 / width) + 1e-05)
        high = root.astype(BF16).astype(F32)
        mid = (root - high).astype(BF16).astype(F32)
        low = root - high - mid
        emb[at, heads * hd : (heads + 1) * hd] = jnp.where(
            lane_chunk == 0,
            high,
            jnp.where(lane_chunk == 1, mid, jnp.where(lane_chunk == 2, low, 0.0)),
        ).astype(BF16)
        return carry

    lax.fori_loop(0, vocab // chunk, table_norm, 0)
    for hh in range(heads):
        emb[:, hh * hd : (hh + 1) * hd] = tbl[:, columns(head_of(me_p, me_s, hh))]

    pl.semaphore_wait(barrier, n_dev - 1)

    for k in range(1, plane):
        p = lax.rem(me_p + k, plane)
        remote(toks.at[me_p], toks.at[me_p], t_send, t_recv, me_z * plane + p, me_s).start()

    my_head = lax.div(me_d * rows, hd)
    to_p = lax.rem(my_head, plane)
    to_i = lax.div(my_head, plane)
    to_s = lax.div(to_i, heads)
    place = lax.rem(to_i, heads) * per_head + lax.rem(me_d, per_head)
    keep = (to_p == me_p) & (to_s == me_s)

    @pl.when(keep)
    def _():
        pltpu.make_async_copy(packed, params.at[me_s, place], w_recv.at[me_s]).start()

    @pl.when(jnp.logical_not(keep))
    def _():
        remote(
            packed,
            params.at[me_s, place],
            w_send,
            w_recv.at[me_s],
            me_z * plane + to_p,
            to_s,
        ).start()

    def give(k, carry):
        z = lax.rem(me_z + k, planes)
        remote(
            packed, params.at[me_s, place], w_send, w_recv.at[me_s], z * plane + to_p, to_s
        ).start()
        return carry

    lax.fori_loop(1, planes, give, 0)

    for k in range(1, plane):
        p = lax.rem(me_p + k, plane)
        for hh in range(heads):
            remote(
                out_grad.at[:, columns(head_of(p, me_s, hh))],
                cot.at[me_p, hh],
                c_send,
                c_recv.at[me_p],
                me_z * plane + p,
                me_s,
            ).start()

    eye = lax.broadcasted_iota(jnp.int32, (seq, seq), 0) == lax.broadcasted_iota(
        jnp.int32, (seq, seq), 1
    )

    def as_column(row):
        return jnp.sum(jnp.where(eye, row, 0.0), axis=1, keepdims=True)

    def exchange(phase, q):
        sums = jnp.sum(acc[...], axis=1, keepdims=True)
        for j in range(slots):
            own = jnp.where(eye, sums[j * seq : (j + 1) * seq], 0.0)
            parts[phase, q, member, j : j + 1, 0:seq] = jnp.sum(own, axis=0, keepdims=True)

        def share(k, carry):
            t = lax.rem(member + k, members)
            remote(
                parts.at[phase, q, member],
                parts.at[phase, q, member],
                x_send,
                x_recv.at[phase, q],
                me_z * plane + lax.div(t, n_sec),
                lax.rem(t, n_sec),
            ).start()
            return carry

        lax.fori_loop(1, members, share, 0)

    def exchanged(phase, q):
        if members > 1:
            whole = parts.at[phase, q, pl.ds(0, members - 1)]
            pltpu.make_async_copy(whole, whole, x_recv.at[phase, q]).wait()
        return jnp.sum(parts[phase, q, :, :, 0:seq], axis=0)

    def layer_param(b, hh):
        at = hh * per_head
        tail = params[b, at, rows:, :].astype(F32)
        weight = params[b, at, :rows, :]
        if per_head > 1:
            for i in range(1, per_head):
                tail = tail + params[b, at + i, rows:, :].astype(F32)
            weight = jnp.concatenate(
                [params[b, at + i, :rows, :] for i in range(per_head)], axis=0
            )
        return weight, tail[0:1], tail[1:2]

    at_row = lax.broadcasted_iota(jnp.int32, (group_rows, group_rows), 0)
    at_col = lax.broadcasted_iota(jnp.int32, (group_rows, group_rows), 1)
    allowed = at_row <= at_col
    for i in range(1, GROUP):
        allowed = allowed & ((at_row >= i * seq) == (at_col >= i * seq))
    vocab_lane = lax.broadcasted_iota(jnp.int32, (seq, vocab), 1).astype(F32)

    if plane > 1:
        pltpu.make_async_copy(
            toks.at[pl.ds(0, plane - 1)], toks.at[pl.ds(0, plane - 1)], t_recv
        ).wait()

    def embed(q, carry):
        for j in range(slots):
            col = as_column(toks[q, j : j + 1, 0:seq])
            picked[j * seq : (j + 1) * seq, :] = jnp.where(vocab_lane == col, 1.0, 0.0).astype(
                BF16
            )
        found = matmul(picked[...], emb[...], 1, 0)
        for hh in range(heads):
            xs[0, q, hh] = found[:, hh * hd : (hh + 1) * hd].astype(BF16)
        root = jnp.sum(found[:, heads * hd :], axis=1, keepdims=True)
        rstd[0, q] = jnp.broadcast_to(root, (slots * seq, hd))
        return carry

    lax.fori_loop(0, plane, embed, 0)

    for b in range(layers):
        pltpu.make_async_copy(params.at[b], params.at[b], w_recv.at[b]).wait()

        def forward(q, carry):
            if b > 0:
                root = lax.rsqrt(exchanged(b - 1, q) * (1.0 / width) + 1e-05)
                for j in range(slots):
                    rstd[b, q, j * seq : (j + 1) * seq, :] = jnp.broadcast_to(
                        as_column(root[j : j + 1]), (seq, hd)
                    )
            held = []
            for hh in range(heads):
                weight, gain_row, scale_row = layer_param(b, hh)
                norm = (xs[b, q, hh].astype(F32) * rstd[b, q] * gain_row).astype(BF16)
                normed[b, q, hh] = norm
                query = (matmul(norm, weight, 1, 0) * inv).astype(BF16)
                queries[b, q, hh] = query
                held.append((norm, query, scale_row))
            tiles = [
                (hh, i, i * group_rows, (i + 1) * group_rows)
                for hh in range(heads)
                for i in range(groups)
            ]
            for some in [tiles[at : at + AHEAD] for at in range(0, len(tiles), AHEAD)]:
                scores = [
                    matmul(held[hh][0][lo:hi], held[hh][1][lo:hi], 1, 1) for hh, i, lo, hi in some
                ]
                scores = [jnp.where(allowed, one, -1e30) for one in scores]
                tops = [jnp.max(one, axis=0, keepdims=True) for one in scores]
                raised = [jnp.exp(one - top) for one, top in zip(scores, tops)]
                sums = [1.0 / jnp.sum(one, axis=0, keepdims=True) for one in raised]
                attends = [one * part for one, part in zip(raised, sums)]
                for (hh, i, lo, hi), attend in zip(some, attends):
                    probs[b, q, hh, i] = attend
                mixes = [
                    matmul(attend.astype(BF16), held[hh][0][lo:hi], 0, 0)
                    for (hh, i, lo, hi), attend in zip(some, attends)
                ]
                for (hh, i, lo, hi), mix in zip(some, mixes):
                    mixed[b, q, hh, lo:hi] = mix
                    if b + 1 < layers:
                        out_rows = xs[b, q, hh, lo:hi].astype(F32) + held[hh][2] * mix
                        out_rows = out_rows.astype(BF16)
                        xs[b + 1, q, hh, lo:hi] = out_rows
                        out_rows = out_rows.astype(F32)
                        if hh == 0:
                            acc[lo:hi] = out_rows * out_rows
                        else:
                            acc[lo:hi] += out_rows * out_rows
            if b + 1 < layers:
                exchange(b, q)
            return carry

        lax.fori_loop(0, plane, forward, 0)

    for b in reversed(range(layers)):
        for hh in range(heads):
            grads[hh] = jnp.zeros((hd, hd), F32)
            tails[hh] = jnp.zeros((8, hd), F32)

        def backward(q, carry):
            if b + 1 == layers:
                pltpu.make_async_copy(cot.at[q], cot.at[q], c_recv.at[q]).wait()
            else:
                phase = layers - 1 + b
                inner = exchanged(phase, q) * (1.0 / width)
                for j in range(slots):
                    at = slice(j * seq, (j + 1) * seq)
                    root = rstd[b + 1, q, at]
                    acc[at] = as_column(inner[j : j + 1]) * root * root * root
                for hh in range(heads):
                    _, gain_row, _ = layer_param(b + 1, hh)
                    dy = dnormed[q, hh].astype(F32) * gain_row
                    back = rstd[b + 1, q] * dy - xs[b + 1, q, hh].astype(F32) * acc[...]
                    cot[q, hh] = (cot[q, hh].astype(F32) + back).astype(BF16)
            for hh in range(heads):
                weight, gain_row, scale_row = layer_param(b, hh)
                given = cot[q, hh].astype(F32)
                scale_part = jnp.sum(given * mixed[b, q, hh], axis=0, keepdims=True)
                norm = normed[b, q, hh]
                query = queries[b, q, hh]
                dmix = (given * scale_row).astype(BF16)
                cuts = [(i, i * group_rows, (i + 1) * group_rows) for i in range(groups)]
                dquery_parts, dnorm_parts = [], []
                for some in [cuts[at : at + AHEAD] for at in range(0, len(cuts), AHEAD)]:
                    datts = [
                        matmul(norm[lo:hi], dmix[lo:hi], 1, 1).astype(BF16).astype(F32)
                        for i, lo, hi in some
                    ]
                    attends = [probs[b, q, hh, i] for i, lo, hi in some]
                    inners = [
                        jnp.sum(datt * attend, axis=0, keepdims=True)
                        for datt, attend in zip(datts, attends)
                    ]
                    dscores = [
                        (attend * (datt - inner)).astype(BF16)
                        for datt, attend, inner in zip(datts, attends, inners)
                    ]
                    dquery_parts += [
                        matmul(dscore, norm[lo:hi], 0, 0).astype(BF16)
                        for (i, lo, hi), dscore in zip(some, dscores)
                    ]
                    dnorm_parts += [
                        matmul(dscore, query[lo:hi], 1, 0)
                        + matmul(attend.astype(BF16), dmix[lo:hi], 1, 0)
                        for (i, lo, hi), dscore, attend in zip(some, dscores, attends)
                    ]
                dquery = jnp.concatenate(dquery_parts, axis=0)
                dnorm = jnp.concatenate(dnorm_parts, axis=0) + matmul(dquery, weight, 1, 1) * inv
                grads[hh] += matmul(norm, dquery, 0, 0)
                dnorm = dnorm.astype(BF16)
                if b > 0:
                    dnormed[q, hh] = dnorm
                dnorm = dnorm.astype(F32)
                x_in = xs[b, q, hh].astype(F32)
                tails[hh, 0:1] += jnp.sum(dnorm * (x_in * rstd[b, q]), axis=0, keepdims=True)
                tails[hh, 1:2] += scale_part
                if b > 0:
                    inside = dnorm * gain_row * x_in
                    if hh == 0:
                        acc[...] = inside
                    else:
                        acc[...] += inside
            if b > 0:
                exchange(layers - 2 + b, q)
            return carry

        lax.fori_loop(0, plane, backward, 0)
        for hh in range(heads):
            gain_part, scale_part = tails[hh, 0:1], tails[hh, 1:2]
            gain_hi = gain_part.astype(BF16).astype(F32)
            scale_hi = scale_part.astype(BF16).astype(F32)
            tail = jnp.where(
                tail_row == 0,
                gain_hi,
                jnp.where(
                    tail_row == 1,
                    gain_part - gain_hi,
                    jnp.where(
                        tail_row == 2,
                        scale_hi,
                        jnp.where(tail_row == 3, scale_part - scale_hi, 0.0),
                    ),
                ),
            ).astype(BF16)
            dweight = (grads[hh] * inv).astype(BF16)
            for i in range(per_head):
                at = hh * per_head + i
                tx[b, at, 0:rows] = dweight[i * rows : (i + 1) * rows]
                tx[b, at, rows : rows + TAIL] = tail
        for hh in range(heads):
            for i in range(per_head):
                at = hh * per_head + i
                r = head_of(me_p, me_s, hh) * per_head + i
                mine = (r == me_d) & (me_s == b)

                @pl.when(mine)
                def _():
                    pltpu.make_async_copy(tx.at[b, at], rx.at[me_z], g_recv).start()

                @pl.when(jnp.logical_not(mine))
                def _():
                    remote(tx.at[b, at], rx.at[me_z], g_send, g_recv, r, b).start()

    pltpu.make_async_copy(rx, rx, g_recv).wait()
    total = jnp.sum(rx[...].astype(F32), axis=0)
    total_query = total[0:rows]
    total_gain = total[rows : rows + 1] + total[rows + 1 : rows + 2]
    total_scale = total[rows + 2 : rows + 3] + total[rows + 3 : rows + 4]
    if per_head > 1:
        at = lax.broadcasted_iota(jnp.int32, (1, hd), 1)
        first = lax.rem(me_d, per_head) * rows
        inside = (at >= first) & (at < first + rows)
        total_gain = jnp.where(inside, total_gain, 0.0)
        total_scale = jnp.where(inside, total_scale, 0.0)
    squares = (
        jnp.sum(total_query * total_query, axis=0, keepdims=True)
        + total_gain * total_gain
        + total_scale * total_scale
    )
    norms[pl.ds(me, 1)] = squares[None]

    def tell(k, carry):
        t = lax.rem(me + k, n_dev)
        remote(
            norms.at[me], norms.at[me], n_send, n_recv, lax.div(t, n_sec), lax.rem(t, n_sec)
        ).start()
        return carry

    lax.fori_loop(1, n_dev, tell, 0)
    others = norms.at[pl.ds(0, n_dev - 1)]
    pltpu.make_async_copy(others, others, n_recv).wait()
    overall = jnp.sum(jnp.sum(norms[...], axis=0), axis=1, keepdims=True)
    limit = float(layers * width * (hd + 2))
    factor = jnp.minimum(1.0, math.sqrt(limit) / jnp.sqrt(overall))
    out[0:rows] = total_query * factor
    out[rows : rows + 8] = jnp.where(
        lax.broadcasted_iota(jnp.int32, (8, hd), 0) == 0, total_gain * factor, total_scale * factor
    )

    pltpu.make_async_copy(others, others, n_send).wait()
    if members > 1:
        for phase in range(2 * layers - 2):
            whole = parts.at[phase, :, pl.ds(0, members - 1)]
            pltpu.make_async_copy(whole, whole, x_send).wait()
    if plane > 1:
        sent = toks.at[pl.ds(0, plane - 1)]
        pltpu.make_async_copy(sent, sent, t_send).wait()
        sent = cot.at[pl.ds(0, plane - 1)]
        pltpu.make_async_copy(sent, sent, c_send).wait()

    def sent_weight(k, carry):
        pltpu.make_async_copy(packed, packed, w_send).wait()
        return carry

    lax.fori_loop(0, jnp.where(keep, planes - 1, planes), sent_weight, 0)

    def sent_grad(k, carry):
        pltpu.make_async_copy(packed, packed, g_send).wait()
        return carry

    pieces = layers * heads * per_head
    lax.fori_loop(0, jnp.where(keep, pieces - 1, pieces), sent_grad, 0)


def on_device(path_table, tokens, assign, out_grad, query_weights, gain, scale):
    n_dp = lax.axis_size("dp")
    n_sec = lax.axis_size("section")
    vocab, width = path_table.shape
    slots, seq = tokens.shape[1:]
    rows, hd = query_weights.shape[1:]
    count = slots * seq
    layers = n_sec
    plane, planes, heads = layout(n_dp, n_sec, width, hd)
    per_head = hd // rows
    pieces = heads * per_head
    n_dev = n_dp * n_sec
    groups = slots // GROUP
    first = lax.rem(lax.axis_index("dp") * rows, hd)
    if rows < hd:
        gain = lax.dynamic_update_slice(jnp.zeros((1, hd), BF16), gain, (0, first))
        scale = lax.dynamic_update_slice(jnp.zeros((1, hd), BF16), scale, (0, first))
    vmem = pl.BlockSpec(memory_space=pltpu.VMEM)
    hbm = pl.BlockSpec(memory_space=pl.ANY)
    smem = pl.BlockSpec(memory_space=pltpu.SMEM)
    found = pl.pallas_call(
        functools.partial(step_kernel, n_dp, n_sec),
        out_shape=jax.ShapeDtypeStruct((rows + 8, hd), F32),
        in_specs=[hbm, vmem, smem, hbm, vmem, vmem, vmem],
        out_specs=vmem,
        scratch_shapes=[
            pltpu.VMEM((rows + TAIL, hd), BF16),
            pltpu.VMEM((layers, pieces, rows + TAIL, hd), BF16),
            pltpu.VMEM((plane, slots, hd), F32),
            pltpu.VMEM((count, vocab), BF16),
            pltpu.VMEM((vocab, width), BF16),
            pltpu.VMEM((vocab, (heads + 1) * hd), BF16),
            pltpu.VMEM((plane, heads, count, hd), BF16),
            pltpu.VMEM((layers, plane, heads, count, hd), BF16),
            pltpu.VMEM((layers, plane, heads, count, hd), BF16),
            pltpu.VMEM((layers, plane, heads, count, hd), BF16),
            pltpu.VMEM((layers, plane, heads, count, hd), F32),
            pltpu.VMEM((layers, plane, heads, groups, GROUP * seq, GROUP * seq), F32),
            pltpu.VMEM((plane, heads, count, hd), BF16),
            pltpu.VMEM((count, hd), F32),
            pltpu.VMEM((layers, plane, count, hd), F32),
            pltpu.VMEM((max(1, 2 * layers - 2), plane, plane * n_sec, slots, hd), F32),
            pltpu.VMEM((heads, hd, hd), F32),
            pltpu.VMEM((heads, 8, hd), F32),
            pltpu.VMEM((layers, pieces, rows + TAIL, hd), BF16),
            pltpu.VMEM((planes, rows + TAIL, hd), BF16),
            pltpu.VMEM((n_dev, 1, hd), F32),
            pltpu.SemaphoreType.DMA,
            pltpu.SemaphoreType.DMA,
            pltpu.SemaphoreType.DMA,
            pltpu.SemaphoreType.DMA,
            pltpu.SemaphoreType.DMA((layers,)),
            pltpu.SemaphoreType.DMA,
            pltpu.SemaphoreType.DMA((plane,)),
            pltpu.SemaphoreType.DMA,
            pltpu.SemaphoreType.DMA((max(1, 2 * layers - 2), plane)),
            pltpu.SemaphoreType.DMA,
            pltpu.SemaphoreType.DMA,
            pltpu.SemaphoreType.DMA,
            pltpu.SemaphoreType.DMA,
        ],
        compiler_params=pltpu.CompilerParams(
            collective_id=0, has_side_effects=True, vmem_limit_bytes=56 * 1024 * 1024
        ),
    )(
        path_table,
        tokens[0],
        assign[0],
        out_grad.reshape(count, width),
        query_weights[0],
        gain,
        scale,
    )
    query_grad = found[:rows]
    gain_grad, scale_grad = found[rows : rows + 1], found[rows + 1 : rows + 2]
    if rows < hd:
        gain_grad = lax.dynamic_slice(gain_grad, (0, first), (1, rows))
        scale_grad = lax.dynamic_slice(scale_grad, (0, first), (1, rows))
    return query_grad[None], gain_grad, scale_grad


def solution(mesh):
    in_specs = (
        P(),
        P("dp", None, None),
        P("dp", None),
        P("dp", None, None, None, None),
        P("section", "dp", None),
        P("section", "dp"),
        P("section", "dp"),
    )
    out_specs = (P("section", "dp", None), P("section", "dp"), P("section", "dp"))
    return jax.shard_map(
        on_device, mesh=mesh, in_specs=in_specs, out_specs=out_specs, check_vma=False
    )
```

```python
import functools
import math

import jax
import jax.numpy as jnp
from jax import lax
from jax.experimental import pallas as pl
from jax.experimental.pallas import tpu as pltpu
from jax.sharding import PartitionSpec as P

MESH = pl.DeviceIdType.MESH
F32 = jnp.float32
BF16 = jnp.bfloat16
TAIL = 16
GROUP = 2
PLANE = 4
AHEAD = 8


def matmul(lhs, rhs, lhs_dim, rhs_dim):
    return lax.dot_general(
        lhs, rhs, (((lhs_dim,), (rhs_dim,)), ((), ())), preferred_element_type=F32
    )


def layout(n_dp, n_sec, width, hd):
    plane = math.gcd(n_dp, min(PLANE, width // hd // n_sec))
    return plane, n_dp // plane, width // hd // n_sec // plane


def step_kernel(
    n_dp,
    n_sec,
    table,
    tokens,
    assign,
    out_grad,
    weights,
    gain,
    scale,
    out,
    packed,
    params,
    toks,
    picked,
    tbl,
    emb,
    cot,
    xs,
    normed,
    queries,
    mixed,
    probs,
    dnormed,
    acc,
    rstd,
    parts,
    grads,
    tails,
    tx,
    rx,
    norms,
    load_sem,
    t_send,
    t_recv,
    w_send,
    w_recv,
    c_send,
    c_recv,
    x_send,
    x_recv,
    g_send,
    g_recv,
    n_send,
    n_recv,
):
    slots, seq = tokens.shape
    vocab, width = table.shape
    rows, hd = weights.shape
    plane, planes, heads = layout(n_dp, n_sec, width, hd)
    layers = n_sec
    per_head = hd // rows
    n_dev = n_dp * n_sec
    members = plane * n_sec
    group_rows = GROUP * seq
    groups = slots // GROUP
    inv = 1.0 / math.sqrt(hd)
    me_d = lax.axis_index("dp")
    me_s = lax.axis_index("section")
    me = me_d * n_sec + me_s
    me_z = lax.div(me_d, plane)
    me_p = lax.rem(me_d, plane)
    member = me_p * n_sec + me_s

    def head_of(p, c, hh):
        return (c * heads + hh) * plane + p

    def columns(h):
        return pl.ds(pl.multiple_of(h * hd, hd), hd)

    def remote(src, dst, ssem, rsem, d, s):
        return pltpu.make_async_remote_copy(
            src_ref=src,
            dst_ref=dst,
            send_sem=ssem,
            recv_sem=rsem,
            device_id=(d, s),
            device_id_type=MESH,
        )

    pltpu.make_async_copy(table, tbl, load_sem).start()
    for hh in range(heads):
        pltpu.make_async_copy(
            out_grad.at[:, columns(head_of(me_p, me_s, hh))], cot.at[me_p, hh], c_recv.at[me_p]
        ).start()

    barrier = pltpu.get_barrier_semaphore()

    def greet(k, carry):
        t = lax.rem(me + k, n_dev)
        pl.semaphore_signal(
            barrier,
            inc=1,
            device_id=(lax.div(t, n_sec), lax.rem(t, n_sec)),
            device_id_type=MESH,
        )
        return carry

    lax.fori_loop(1, n_dev, greet, 0)

    packed[0:rows, :] = weights[...]
    tail_row = lax.broadcasted_iota(jnp.int32, (TAIL, hd), 0)
    packed[rows : rows + TAIL, :] = jnp.where(
        tail_row == 0,
        gain[...].astype(F32),
        jnp.where(tail_row == 1, scale[...].astype(F32), 0.0),
    ).astype(BF16)
    for j in range(slots):
        toks[me_p, j : j + 1, 0:seq] = tokens[pl.ds(assign[j], 1), :].astype(F32)

    pltpu.make_async_copy(tbl, tbl, load_sem).wait()
    chunk = math.gcd(vocab, 64)
    lane_chunk = lax.broadcasted_iota(jnp.int32, (chunk, hd), 1)

    def table_norm(i, carry):
        at = pl.ds(pl.multiple_of(i * chunk, chunk), chunk)
        squares = jnp.zeros((chunk, hd), F32)
        for h in range(width // hd):
            block = tbl[at, h * hd : (h + 1) * hd].astype(F32)
            squares = squares + block * block
        root = lax.rsqrt(jnp.sum(squares, axis=1, keepdims=True) * (1.0 / width) + 1e-05)
        high = root.astype(BF16).astype(F32)
        mid = (root - high).astype(BF16).astype(F32)
        low = root - high - mid
        emb[at, heads * hd : (heads + 1) * hd] = jnp.where(
            lane_chunk == 0,
            high,
            jnp.where(lane_chunk == 1, mid, jnp.where(lane_chunk == 2, low, 0.0)),
        ).astype(BF16)
        return carry

    lax.fori_loop(0, vocab // chunk, table_norm, 0)
    for hh in range(heads):
        emb[:, hh * hd : (hh + 1) * hd] = tbl[:, columns(head_of(me_p, me_s, hh))]

    pl.semaphore_wait(barrier, n_dev - 1)

    for k in range(1, plane):
        p = lax.rem(me_p + k, plane)
        remote(toks.at[me_p], toks.at[me_p], t_send, t_recv, me_z * plane + p, me_s).start()

    my_head = lax.div(me_d * rows, hd)
    to_p = lax.rem(my_head, plane)
    to_i = lax.div(my_head, plane)
    to_s = lax.div(to_i, heads)
    place = lax.rem(to_i, heads) * per_head + lax.rem(me_d, per_head)
    keep = (to_p == me_p) & (to_s == me_s)

    @pl.when(keep)
    def _():
        pltpu.make_async_copy(packed, params.at[me_s, place], w_recv.at[me_s]).start()

    @pl.when(jnp.logical_not(keep))
    def _():
        remote(
            packed,
            params.at[me_s, place],
            w_send,
            w_recv.at[me_s],
            me_z * plane + to_p,
            to_s,
        ).start()

    def give(k, carry):
        z = lax.rem(me_z + k, planes)
        remote(
            packed, params.at[me_s, place], w_send, w_recv.at[me_s], z * plane + to_p, to_s
        ).start()
        return carry

    lax.fori_loop(1, planes, give, 0)

    for k in range(1, plane):
        p = lax.rem(me_p + k, plane)
        for hh in range(heads):
            remote(
                out_grad.at[:, columns(head_of(p, me_s, hh))],
                cot.at[me_p, hh],
                c_send,
                c_recv.at[me_p],
                me_z * plane + p,
                me_s,
            ).start()

    eye = lax.broadcasted_iota(jnp.int32, (seq, seq), 0) == lax.broadcasted_iota(
        jnp.int32, (seq, seq), 1
    )

    def as_column(row):
        return jnp.sum(jnp.where(eye, row, 0.0), axis=1, keepdims=True)

    def exchange(phase, q):
        sums = jnp.sum(acc[...], axis=1, keepdims=True)
        for j in range(slots):
            own = jnp.where(eye, sums[j * seq : (j + 1) * seq], 0.0)
            parts[phase, q, member, j : j + 1, 0:seq] = jnp.sum(own, axis=0, keepdims=True)

        def share(k, carry):
            t = lax.rem(member + k, members)
            remote(
                parts.at[phase, q, member],
                parts.at[phase, q, member],
                x_send,
                x_recv.at[phase, q],
                me_z * plane + lax.div(t, n_sec),
                lax.rem(t, n_sec),
            ).start()
            return carry

        lax.fori_loop(1, members, share, 0)

    def exchanged(phase, q):
        if members > 1:
            whole = parts.at[phase, q, pl.ds(0, members - 1)]
            pltpu.make_async_copy(whole, whole, x_recv.at[phase, q]).wait()
        return jnp.sum(parts[phase, q, :, :, 0:seq], axis=0)

    def layer_param(b, hh):
        at = hh * per_head
        tail = params[b, at, rows:, :].astype(F32)
        weight = params[b, at, :rows, :]
        if per_head > 1:
            for i in range(1, per_head):
                tail = tail + params[b, at + i, rows:, :].astype(F32)
            weight = jnp.concatenate(
                [params[b, at + i, :rows, :] for i in range(per_head)], axis=0
            )
        return weight, tail[0:1], tail[1:2]

    at_row = lax.broadcasted_iota(jnp.int32, (group_rows, group_rows), 0)
    at_col = lax.broadcasted_iota(jnp.int32, (group_rows, group_rows), 1)
    allowed = at_row <= at_col
    for i in range(1, GROUP):
        allowed = allowed & ((at_row >= i * seq) == (at_col >= i * seq))
    vocab_lane = lax.broadcasted_iota(jnp.int32, (seq, vocab), 1).astype(F32)

    if plane > 1:
        pltpu.make_async_copy(
            toks.at[pl.ds(0, plane - 1)], toks.at[pl.ds(0, plane - 1)], t_recv
        ).wait()

    def embed(q, carry):
        for j in range(slots):
            col = as_column(toks[q, j : j + 1, 0:seq])
            picked[j * seq : (j + 1) * seq, :] = jnp.where(vocab_lane == col, 1.0, 0.0).astype(
                BF16
            )
        found = matmul(picked[...], emb[...], 1, 0)
        for hh in range(heads):
            xs[0, q, hh] = found[:, hh * hd : (hh + 1) * hd].astype(BF16)
        root = jnp.sum(found[:, heads * hd :], axis=1, keepdims=True)
        rstd[0, q] = jnp.broadcast_to(root, (slots * seq, hd))
        return carry

    lax.fori_loop(0, plane, embed, 0)

    for b in range(layers):
        pltpu.make_async_copy(params.at[b], params.at[b], w_recv.at[b]).wait()

        def forward(q, carry):
            if b > 0:
                root = lax.rsqrt(exchanged(b - 1, q) * (1.0 / width) + 1e-05)
                for j in range(slots):
                    rstd[b, q, j * seq : (j + 1) * seq, :] = jnp.broadcast_to(
                        as_column(root[j : j + 1]), (seq, hd)
                    )
            held = []
            for hh in range(heads):
                weight, gain_row, scale_row = layer_param(b, hh)
                norm = (xs[b, q, hh].astype(F32) * rstd[b, q] * gain_row).astype(BF16)
                normed[b, q, hh] = norm
                query = (matmul(norm, weight, 1, 0) * inv).astype(BF16)
                queries[b, q, hh] = query
                held.append((norm, query, scale_row))
            tiles = [
                (hh, i, i * group_rows, (i + 1) * group_rows)
                for hh in range(heads)
                for i in range(groups)
            ]
            for some in [tiles[at : at + AHEAD] for at in range(0, len(tiles), AHEAD)]:
                scores = [
                    matmul(held[hh][0][lo:hi], held[hh][1][lo:hi], 1, 1) for hh, i, lo, hi in some
                ]
                scores = [jnp.where(allowed, one, -1e30) for one in scores]
                tops = [jnp.max(one, axis=0, keepdims=True) for one in scores]
                raised = [jnp.exp(one - top) for one, top in zip(scores, tops)]
                sums = [1.0 / jnp.sum(one, axis=0, keepdims=True) for one in raised]
                attends = [one * part for one, part in zip(raised, sums)]
                for (hh, i, lo, hi), attend in zip(some, attends):
                    probs[b, q, hh, i] = attend
                mixes = [
                    matmul(attend.astype(BF16), held[hh][0][lo:hi], 0, 0)
                    for (hh, i, lo, hi), attend in zip(some, attends)
                ]
                for (hh, i, lo, hi), mix in zip(some, mixes):
                    mixed[b, q, hh, lo:hi] = mix
                    if b + 1 < layers:
                        out_rows = xs[b, q, hh, lo:hi].astype(F32) + held[hh][2] * mix
                        out_rows = out_rows.astype(BF16)
                        xs[b + 1, q, hh, lo:hi] = out_rows
                        out_rows = out_rows.astype(F32)
                        if hh == 0:
                            acc[lo:hi] = out_rows * out_rows
                        else:
                            acc[lo:hi] += out_rows * out_rows
            if b + 1 < layers:
                exchange(b, q)
            return carry

        lax.fori_loop(0, plane, forward, 0)

    for b in reversed(range(layers)):
        for hh in range(heads):
            grads[hh] = jnp.zeros((hd, hd), F32)
            tails[hh] = jnp.zeros((8, hd), F32)

        def backward(q, carry):
            if b + 1 == layers:
                pltpu.make_async_copy(cot.at[q], cot.at[q], c_recv.at[q]).wait()
            else:
                phase = layers - 1 + b
                inner = exchanged(phase, q) * (1.0 / width)
                for j in range(slots):
                    at = slice(j * seq, (j + 1) * seq)
                    root = rstd[b + 1, q, at]
                    acc[at] = as_column(inner[j : j + 1]) * root * root * root
                for hh in range(heads):
                    _, gain_row, _ = layer_param(b + 1, hh)
                    dy = dnormed[q, hh].astype(F32) * gain_row
                    back = rstd[b + 1, q] * dy - xs[b + 1, q, hh].astype(F32) * acc[...]
                    cot[q, hh] = (cot[q, hh].astype(F32) + back).astype(BF16)
            held = []
            for hh in range(heads):
                weight, gain_row, scale_row = layer_param(b, hh)
                given = cot[q, hh].astype(F32)
                tails[hh, 1:2] += jnp.sum(given * mixed[b, q, hh], axis=0, keepdims=True)
                held.append((weight, gain_row, (given * scale_row).astype(BF16)))
            dqueries, dnorms = [], []
            for hh in range(heads):
                dmix = held[hh][2]
                cuts = [(i, i * group_rows, (i + 1) * group_rows) for i in range(groups)]
                datts = [
                    matmul(normed[b, q, hh, lo:hi], dmix[lo:hi], 1, 1)
                    .astype(BF16)
                    .astype(F32)
                    for i, lo, hi in cuts
                ]
                attends = [probs[b, q, hh, i] for i, lo, hi in cuts]
                inners = [
                    jnp.sum(datt * attend, axis=0, keepdims=True)
                    for datt, attend in zip(datts, attends)
                ]
                dscores = [
                    (attend * (datt - inner)).astype(BF16)
                    for datt, attend, inner in zip(datts, attends, inners)
                ]
                dqueries.append(
                    [
                        matmul(dscore, normed[b, q, hh, lo:hi], 0, 0).astype(BF16)
                        for (i, lo, hi), dscore in zip(cuts, dscores)
                    ]
                )
                dnorms.append(
                    [
                        matmul(dscore, queries[b, q, hh, lo:hi], 1, 0)
                        + matmul(attend.astype(BF16), dmix[lo:hi], 1, 0)
                        for (i, lo, hi), dscore, attend in zip(cuts, dscores, attends)
                    ]
                )
            for hh in range(heads):
                weight, gain_row, _ = held[hh]
                dquery = jnp.concatenate(dqueries[hh], axis=0)
                dnorm = jnp.concatenate(dnorms[hh], axis=0) + matmul(dquery, weight, 1, 1) * inv
                grads[hh] += matmul(normed[b, q, hh], dquery, 0, 0)
                dnorm = dnorm.astype(BF16)
                if b > 0:
                    dnormed[q, hh] = dnorm
                dnorm = dnorm.astype(F32)
                x_in = xs[b, q, hh].astype(F32)
                tails[hh, 0:1] += jnp.sum(dnorm * (x_in * rstd[b, q]), axis=0, keepdims=True)
                if b > 0:
                    inside = dnorm * gain_row * x_in
                    if hh == 0:
                        acc[...] = inside
                    else:
                        acc[...] += inside
            if b > 0:
                exchange(layers - 2 + b, q)
            return carry

        lax.fori_loop(0, plane, backward, 0)
        for hh in range(heads):
            gain_part, scale_part = tails[hh, 0:1], tails[hh, 1:2]
            gain_hi = gain_part.astype(BF16).astype(F32)
            scale_hi = scale_part.astype(BF16).astype(F32)
            tail = jnp.where(
                tail_row == 0,
                gain_hi,
                jnp.where(
                    tail_row == 1,
                    gain_part - gain_hi,
                    jnp.where(
                        tail_row == 2,
                        scale_hi,
                        jnp.where(tail_row == 3, scale_part - scale_hi, 0.0),
                    ),
                ),
            ).astype(BF16)
            dweight = (grads[hh] * inv).astype(BF16)
            for i in range(per_head):
                at = hh * per_head + i
                tx[b, at, 0:rows] = dweight[i * rows : (i + 1) * rows]
                tx[b, at, rows : rows + TAIL] = tail
        for hh in range(heads):
            for i in range(per_head):
                at = hh * per_head + i
                r = head_of(me_p, me_s, hh) * per_head + i
                mine = (r == me_d) & (me_s == b)

                @pl.when(mine)
                def _():
                    pltpu.make_async_copy(tx.at[b, at], rx.at[me_z], g_recv).start()

                @pl.when(jnp.logical_not(mine))
                def _():
                    remote(tx.at[b, at], rx.at[me_z], g_send, g_recv, r, b).start()

    pltpu.make_async_copy(rx, rx, g_recv).wait()
    total = jnp.sum(rx[...].astype(F32), axis=0)
    total_query = total[0:rows]
    total_gain = total[rows : rows + 1] + total[rows + 1 : rows + 2]
    total_scale = total[rows + 2 : rows + 3] + total[rows + 3 : rows + 4]
    if per_head > 1:
        at = lax.broadcasted_iota(jnp.int32, (1, hd), 1)
        first = lax.rem(me_d, per_head) * rows
        inside = (at >= first) & (at < first + rows)
        total_gain = jnp.where(inside, total_gain, 0.0)
        total_scale = jnp.where(inside, total_scale, 0.0)
    squares = (
        jnp.sum(total_query * total_query, axis=0, keepdims=True)
        + total_gain * total_gain
        + total_scale * total_scale
    )
    norms[pl.ds(me, 1)] = squares[None]

    def tell(k, carry):
        t = lax.rem(me + k, n_dev)
        remote(
            norms.at[me], norms.at[me], n_send, n_recv, lax.div(t, n_sec), lax.rem(t, n_sec)
        ).start()
        return carry

    lax.fori_loop(1, n_dev, tell, 0)
    others = norms.at[pl.ds(0, n_dev - 1)]
    pltpu.make_async_copy(others, others, n_recv).wait()
    overall = jnp.sum(jnp.sum(norms[...], axis=0), axis=1, keepdims=True)
    limit = float(layers * width * (hd + 2))
    factor = jnp.minimum(1.0, math.sqrt(limit) / jnp.sqrt(overall))
    out[0:rows] = total_query * factor
    out[rows : rows + 8] = jnp.where(
        lax.broadcasted_iota(jnp.int32, (8, hd), 0) == 0, total_gain * factor, total_scale * factor
    )

    pltpu.make_async_copy(others, others, n_send).wait()
    if members > 1:
        for phase in range(2 * layers - 2):
            whole = parts.at[phase, :, pl.ds(0, members - 1)]
            pltpu.make_async_copy(whole, whole, x_send).wait()
    if plane > 1:
        sent = toks.at[pl.ds(0, plane - 1)]
        pltpu.make_async_copy(sent, sent, t_send).wait()
        sent = cot.at[pl.ds(0, plane - 1)]
        pltpu.make_async_copy(sent, sent, c_send).wait()

    def sent_weight(k, carry):
        pltpu.make_async_copy(packed, packed, w_send).wait()
        return carry

    lax.fori_loop(0, jnp.where(keep, planes - 1, planes), sent_weight, 0)

    def sent_grad(k, carry):
        pltpu.make_async_copy(packed, packed, g_send).wait()
        return carry

    pieces = layers * heads * per_head
    lax.fori_loop(0, jnp.where(keep, pieces - 1, pieces), sent_grad, 0)


def on_device(path_table, tokens, assign, out_grad, query_weights, gain, scale):
    n_dp = lax.axis_size("dp")
    n_sec = lax.axis_size("section")
    vocab, width = path_table.shape
    slots, seq = tokens.shape[1:]
    rows, hd = query_weights.shape[1:]
    count = slots * seq
    layers = n_sec
    plane, planes, heads = layout(n_dp, n_sec, width, hd)
    per_head = hd // rows
    pieces = heads * per_head
    n_dev = n_dp * n_sec
    groups = slots // GROUP
    first = lax.rem(lax.axis_index("dp") * rows, hd)
    if rows < hd:
        gain = lax.dynamic_update_slice(jnp.zeros((1, hd), BF16), gain, (0, first))
        scale = lax.dynamic_update_slice(jnp.zeros((1, hd), BF16), scale, (0, first))
    vmem = pl.BlockSpec(memory_space=pltpu.VMEM)
    hbm = pl.BlockSpec(memory_space=pl.ANY)
    smem = pl.BlockSpec(memory_space=pltpu.SMEM)
    found = pl.pallas_call(
        functools.partial(step_kernel, n_dp, n_sec),
        out_shape=jax.ShapeDtypeStruct((rows + 8, hd), F32),
        in_specs=[hbm, vmem, smem, hbm, vmem, vmem, vmem],
        out_specs=vmem,
        scratch_shapes=[
            pltpu.VMEM((rows + TAIL, hd), BF16),
            pltpu.VMEM((layers, pieces, rows + TAIL, hd), BF16),
            pltpu.VMEM((plane, slots, hd), F32),
            pltpu.VMEM((count, vocab), BF16),
            pltpu.VMEM((vocab, width), BF16),
            pltpu.VMEM((vocab, (heads + 1) * hd), BF16),
            pltpu.VMEM((plane, heads, count, hd), BF16),
            pltpu.VMEM((layers, plane, heads, count, hd), BF16),
            pltpu.VMEM((layers, plane, heads, count, hd), BF16),
            pltpu.VMEM((layers, plane, heads, count, hd), BF16),
            pltpu.VMEM((layers, plane, heads, count, hd), F32),
            pltpu.VMEM((layers, plane, heads, groups, GROUP * seq, GROUP * seq), F32),
            pltpu.VMEM((plane, heads, count, hd), BF16),
            pltpu.VMEM((count, hd), F32),
            pltpu.VMEM((layers, plane, count, hd), F32),
            pltpu.VMEM((max(1, 2 * layers - 2), plane, plane * n_sec, slots, hd), F32),
            pltpu.VMEM((heads, hd, hd), F32),
            pltpu.VMEM((heads, 8, hd), F32),
            pltpu.VMEM((layers, pieces, rows + TAIL, hd), BF16),
            pltpu.VMEM((planes, rows + TAIL, hd), BF16),
            pltpu.VMEM((n_dev, 1, hd), F32),
            pltpu.SemaphoreType.DMA,
            pltpu.SemaphoreType.DMA,
            pltpu.SemaphoreType.DMA,
            pltpu.SemaphoreType.DMA,
            pltpu.SemaphoreType.DMA((layers,)),
            pltpu.SemaphoreType.DMA,
            pltpu.SemaphoreType.DMA((plane,)),
            pltpu.SemaphoreType.DMA,
            pltpu.SemaphoreType.DMA((max(1, 2 * layers - 2), plane)),
            pltpu.SemaphoreType.DMA,
            pltpu.SemaphoreType.DMA,
            pltpu.SemaphoreType.DMA,
            pltpu.SemaphoreType.DMA,
        ],
        compiler_params=pltpu.CompilerParams(
            collective_id=0, has_side_effects=True, vmem_limit_bytes=56 * 1024 * 1024
        ),
    )(
        path_table,
        tokens[0],
        assign[0],
        out_grad.reshape(count, width),
        query_weights[0],
        gain,
        scale,
    )
    query_grad = found[:rows]
    gain_grad, scale_grad = found[rows : rows + 1], found[rows + 1 : rows + 2]
    if rows < hd:
        gain_grad = lax.dynamic_slice(gain_grad, (0, first), (1, rows))
        scale_grad = lax.dynamic_slice(scale_grad, (0, first), (1, rows))
    return query_grad[None], gain_grad, scale_grad


def solution(mesh):
    in_specs = (
        P(),
        P("dp", None, None),
        P("dp", None),
        P("dp", None, None, None, None),
        P("section", "dp", None),
        P("section", "dp"),
        P("section", "dp"),
    )
    out_specs = (P("section", "dp", None), P("section", "dp"), P("section", "dp"))
    return jax.shard_map(
        on_device, mesh=mesh, in_specs=in_specs, out_specs=out_specs, check_vma=False
    )
```
